32 devices in a mesh: groups: 1, dev: 16 (over z, y, core), sub: 2 (over x).
Axes of the slice: x: 2, y: 2, z: 4, core: 2. Of those that a mesh axis runs over, the one named last changes fastest.
Arguments:
- stream_in: bfloat16 [2048, 4096], P(('groups', 'dev')), may hold values from -25 to 25
- routes: int32 [2048, 8], P(('groups', 'dev')), may hold values from 0 to 15, all different within a row; in each aligned block of 128 rows (0 to 127, 128 to 255, ...) at most 80 rows name the same one
- route_weight: float32 [2048, 8], P(('groups', 'dev')), may hold values from 0.1 to 1
- gain_one: float32 [4096], replicated, may hold values from 0.5 to 1.5
- gain_two: float32 [4096], replicated, may hold values from 0.5 to 1.5
- w_in: bfloat16 [16, 2, 1536, 4096], P('dev', None, 'sub'), may hold values from -0.09375 to 0.09375
- w_out: bfloat16 [16, 1536, 4096], P('dev', 'sub'), may hold values from -0.15625 to 0.15625
- w_kv: bfloat16 [4096, 1024], P(None, 'sub'), may hold values from -0.09375 to 0.09375
Outputs:
- stream_out: bfloat16 [2048, 4096], P(('groups', 'dev'), 'sub')
- kv_next: bfloat16 [2048, 1024], P(('groups', 'dev'), 'sub')
The draws below stay inside these ranges and needn't reach their ends.
Inputs may be any that keep to these rules, and one draw needn't show every extreme that they name: `routes`: each row names 8 different experts. Among the 128 tokens of one index of dev (aligned blocks of rows) no expert is named more than 80 times, a bound that some block reaches.
All inputs are finite; a program needn't handle non-finite values.
Results may differ from the reference program's by a relative error of at most 0.011.
Values may be sent and summed in bfloat16 or wider, within the bound.
No kernel may reach another device: no remote copies, remote signals or barrier semaphores. Data moves between devices by JAX's collectives and lax.ppermute only.
A program may use at most 128 MiB of HBM per device.

```python
import math
import jax
import jax.numpy as jnp
import numpy as np
from jax import lax

D = 4096
FF = 1536
KV_WIDTH = 1024
TOP = 8
TOK_DEV = 128
EXPERTS = 16
TOKENS = 2048
CAP = 80
N_DEV = 16
N_SUB = 2


def draw_stream_in(key, part):
    key_base, key_rows, key_cols = jax.random.split(key, 3)
    row_scale = jnp.exp(jax.random.uniform(key_rows, (TOKENS, 1), minval=math.log(0.3), maxval=math.log(3.0)))
    col_scale = jnp.exp(jax.random.uniform(key_cols, (1, D), minval=-0.7, maxval=0.7))
    base = jnp.clip(jax.random.normal(key_base, (TOKENS, D)), -4.0, 4.0)
    return (base * row_scale * col_scale).astype(jnp.bfloat16)


def levels(key, dims, cuts, low, high):
    loudness, own = 1.0, jax.random.fold_in(key, 6)
    for dim, blocks in cuts:
        draws = jnp.exp(jax.random.uniform(jax.random.fold_in(own, dim), (blocks,), jnp.float32, low / len(cuts), high / len(cuts)))
        loudness = loudness * jnp.repeat(draws, dims[dim] // blocks).reshape([-1 if axis == dim else 1 for axis in range(len(dims))])
    return loudness


def routed_block(key, own, number, rows, count, top, bound, lean):
    ranking = jax.random.permutation(key, count)
    heavy_load, usual = portions_of(count, rows * top, bound, lean, True), portions_of(count, rows * top, bound, lean, False)
    places = jnp.arange(count)

    def named(sizes, offset_by):
        used = int((sizes > 0).sum())
        fixed = max(1, used // 4)
        passed = fixed + (places - fixed + offset_by * (used - fixed)) % max(1, count - fixed)
        return jnp.zeros((count,), jnp.int32).at[ranking[jnp.where(places < fixed, places, passed)]].set(jnp.asarray(sizes, jnp.int32))

    sizes = jnp.where(number % 4 == 0, named(heavy_load, number // 4), named(usual, number - number // 4 - 1))
    mixed = jax.random.permutation(jax.random.fold_in(own, 3), count)
    giver, taker = mixed[0:count // 2 * 2:2], mixed[1:count // 2 * 2:2]
    slack = jnp.minimum(sizes[giver] - 1, bound - sizes[taker]) // 2
    slack = jnp.where((giver == ranking[0]) | (taker == ranking[0]) | (sizes[taker] == 0), 0, jnp.maximum(slack, 0))
    passed = jax.random.randint(jax.random.fold_in(own, 4), (count // 2,), 0, 1 << 20) % (slack + 1)
    sizes = sizes.at[giver].add(-passed).at[taker].add(passed)
    labels = jnp.searchsorted(jnp.cumsum(sizes), jnp.arange(rows * top), side="right").astype(jnp.int32)
    listing = labels.reshape(top, rows).T
    listing = listing[jax.random.permutation(jax.random.fold_in(own, 1), rows)]
    offset_by = jax.random.randint(jax.random.fold_in(own, 2), (rows, 1), 0, top)
    return jnp.take_along_axis(listing, (jnp.arange(top)[None, :] + offset_by) % top, axis=1)


def portions_of(count, total, limit, slope, full):
    loads = [(1 << 20) // math.isqrt(rank ** slope) + 1 for rank in range(1, count + 1)]
    largest = limit if full else min(limit, max(-(-total // count), total * loads[0] // sum(loads)))
    least = 1 if total - largest >= count - 1 else 0
    holding, rest = [largest] + [least] * (count - 1), total - largest - least * (count - 1)
    while rest > 0:
        candidates = [i for i in range(1, count) if holding[i] < largest] or [i for i in range(1, count) if holding[i] < limit]
        mass, left = sum([loads[i] for i in candidates]), rest
        for i in candidates:
            extra = min(limit - holding[i], max(1, left * loads[i] // mass), rest)
            holding[i] = holding[i] + extra
            rest = rest - extra
    return np.array(holding)


def normal_values(stream_key, extent, width, reach, pieces=(), kind=jnp.bfloat16):
    array = width * jax.random.normal(stream_key, extent, jnp.float32)
    if pieces:
        array = array * levels(stream_key, extent, pieces, -0.22, 0.18)
    return jnp.clip(array, -reach, reach).astype(kind)


def setup_inputs(seed: int = 0, part: int = 0) -> dict:
    arg_keys = jax.random.split(jax.random.key(seed), 9)
    own_keys = jax.random.split(jax.random.fold_in(arg_keys[8], part), 9)
    stream_in = draw_stream_in(jax.random.fold_in(jax.random.fold_in(arg_keys[8], part), 71), part)
    routes_keys = jax.random.split(jax.random.fold_in(own_keys[1], 1), TOKENS // TOK_DEV)
    routes_turns = jax.random.permutation(jax.random.fold_in(own_keys[1], 3), TOKENS // TOK_DEV)
    routes = jax.vmap(lambda own, number: routed_block(jax.random.fold_in(own_keys[1], 2), own, number, TOK_DEV, EXPERTS, TOP, CAP, 2))(routes_keys, routes_turns).reshape((TOKENS, TOP))
    route_weight = jnp.clip(jnp.exp(math.log(1.0) - 2.3025851 * jax.random.uniform(own_keys[2], (TOKENS, TOP), jnp.float32) ** levels(own_keys[2], (TOKENS, TOP), ((0, 16),), -0.2, 0.2)), 0.1, 1.0)
    gain_one = jnp.clip(1.0 + 0.1 * jax.random.normal(arg_keys[3], (D,), jnp.float32), 0.5, 1.5)
    gain_two = jnp.clip(1.0 + 0.1 * jax.random.normal(arg_keys[4], (D,), jnp.float32), 0.5, 1.5)
    w_in = normal_values(arg_keys[5], (EXPERTS, 2, FF, D), D ** -0.5, 0.09375, ((0, 16), (2, 2)))
    w_out = normal_values(arg_keys[6], (EXPERTS, FF, D), FF ** -0.5, 0.15625, ((0, 16), (1, 2)))
    w_kv = normal_values(arg_keys[7], (D, KV_WIDTH), D ** -0.5, 0.09375, ((1, 2),))
    return {"stream_in": stream_in, "routes": routes, "route_weight": route_weight, "gain_one": gain_one, "gain_two": gain_two, "w_in": w_in, "w_out": w_out, "w_kv": w_kv}


EPS = 1e-06

def rms_scale(values, gain_vec):
    mean_square = lax.optimization_barrier(jnp.mean(values * values, axis=-1, keepdims=True))
    return values * lax.rsqrt(mean_square + EPS) * gain_vec

def reference(stream_in, routes, route_weight, gain_one, gain_two, w_in, w_out, w_kv):
    stream_float = stream_in.astype(jnp.float32)
    normed = rms_scale(stream_float, gain_one).astype(jnp.bfloat16)
    flat_routes = routes.reshape(-1).astype(jnp.int32)
    flat_weight = route_weight.reshape(-1)
    most_rows = N_DEV * CAP
    block_size = FF // N_SUB

    def per_expert(accumulated, expert_id):
        matches = flat_routes == expert_id
        picks = jnp.nonzero(matches, size=most_rows, fill_value=0)[0].astype(jnp.int32)
        live_mask = (jnp.arange(most_rows, dtype=jnp.int32) < jnp.sum(matches.astype(jnp.int32))).astype(jnp.float32)
        token_index = (picks // TOP).astype(jnp.int32)
        row_block = normed[token_index]
        gate = jnp.dot(row_block, w_in[expert_id, 0].T, preferred_element_type=jnp.float32)
        up_part = jnp.dot(row_block, w_in[expert_id, 1].T, preferred_element_type=jnp.float32)
        active = (jax.nn.silu(gate) * up_part).astype(jnp.bfloat16)
        down_rows = w_out[expert_id]
        total = jnp.zeros((most_rows, D), jnp.float32)
        for sub_part in range(N_SUB):
            lower = sub_part * block_size
            partial_value = jnp.dot(active[:, lower:lower + block_size], down_rows[lower:lower + block_size], preferred_element_type=jnp.float32).astype(jnp.bfloat16)
            total = total + partial_value.astype(jnp.float32)
        expert_out = total.astype(jnp.bfloat16).astype(jnp.float32)
        scaled = expert_out * (flat_weight[picks] * live_mask)[:, None]
        accumulated = accumulated.at[token_index].add(scaled)
        return (accumulated, None)
    mixture, _ = lax.scan(per_expert, jnp.zeros((TOKENS, D), jnp.float32), jnp.arange(EXPERTS, dtype=jnp.int32))
    stream_out = (stream_float + mixture).astype(jnp.bfloat16)
    normed_next = rms_scale(stream_out.astype(jnp.float32), gain_two).astype(jnp.bfloat16)
    kv_next = jnp.dot(normed_next, w_kv, preferred_element_type=jnp.float32).astype(jnp.bfloat16)
    return (stream_out, kv_next)
```

```python
import functools

import jax
import jax.numpy as jnp
from jax import lax
from jax.experimental import pallas as pl
from jax.experimental.pallas import tpu as pltpu
from jax.sharding import PartitionSpec as P

EPS = 1e-06
BF = jnp.bfloat16
F32 = jnp.float32
LANES = 128
VMEM_LIMIT = 60 * 1024 * 1024


PLAN = (("A", 1), ("B", 1), ("A", 1), ("A", 1))


def vmem():
    return pl.BlockSpec(memory_space=pltpu.VMEM)


def smem():
    return pl.BlockSpec(memory_space=pltpu.SMEM)


def hbm():
    return pl.BlockSpec(memory_space=pl.ANY)


def params():
    return pltpu.CompilerParams(vmem_limit_bytes=VMEM_LIMIT)


def part_of(sub, step, parts):
    return lax.rem(sub + parts - step, parts)


def norm_kernel(chunks, parts, experts, place, x_ref, routes_ref, weight_ref, gain_ref, *outs):
    sub = place[0]
    rows, width = x_ref.shape
    part_width = width // parts
    columns = lax.broadcasted_iota(jnp.int32, (rows, LANES), 1)
    table = jnp.zeros((rows, LANES), F32)
    for k in range(routes_ref.shape[1]):
        table = table + jnp.where(routes_ref[:, k : k + 1] == columns, weight_ref[:, k : k + 1], 0.0)
    outs[0][...] = table
    at = 1
    for kind, first, count in chunks:
        values = x_ref[first : first + count, :].astype(F32)
        scale = lax.rsqrt(jnp.mean(values * values, axis=-1, keepdims=True) + EPS)
        if kind == "B":
            outs[at][...] = (values * scale * gain_ref[...]).astype(BF)
            at += 1
            continue
        for step in range(parts):
            begin = pl.multiple_of(part_of(sub, step, parts) * part_width, part_width)
            piece = x_ref[first : first + count, pl.ds(begin, part_width)].astype(F32)
            outs[at][...] = (piece * scale * gain_ref[:, pl.ds(begin, part_width)]).astype(BF)
            at += 1


def expert_kernel(kind, ring, count, first, parts, place, table_ref, *refs):
    sub, dev = place[0], place[1]
    half = ring * count
    n_in = 2 + 3 * (parts - 1) if kind == "A" else 3
    pieces, refs = refs[:n_in], refs[n_in:]
    win_a, win_b, wout_a, wout_b = refs[:4]
    n_out = 2 * parts if kind == "A" else 2
    outs, refs = refs[4 : 4 + n_out], refs[4 + n_out :]
    x, win, wout, stage, active, in_sem, win_sem, wout_sem, out_sem = refs
    width = x.shape[1]
    part_width = width // parts
    hidden = wout.shape[1]

    def span(step):
        begin = pl.multiple_of(part_of(sub, step, parts) * part_width, part_width)
        return pl.ds(begin, part_width)

    copies = []

    def bring(piece, row, rows, columns):
        copy = pltpu.make_async_copy(
            piece, x.at[pl.ds(row, rows), columns], in_sem.at[len(copies)]
        )
        copy.start()
        copies.append(copy)

    if kind == "A":
        bring(pieces[0], 0, half, span(0))
        bring(pieces[1], half, half, span(0))
        for step in range(1, parts):
            own, along, across = pieces[2 + 3 * (step - 1) : 5 + 3 * (step - 1)]
            bring(own, 0, count, span(step))
            bring(along, count, half - count, span(step))
            bring(across, half, half, span(step))
    else:
        bring(pieces[0], 0, half, pl.ds(0, width))
        bring(pieces[1], half, count, pl.ds(0, width))
        bring(pieces[2], half + count, half - count, pl.ds(0, width))
    tile = hidden
    for candidate in (256, 128):
        if hidden % candidate == 0:
            tile = candidate
            break
    tiles = hidden // tile
    win_copies, wout_copies = [], []
    for expert, source in enumerate((win_a, win_b)):
        for t in range(tiles):
            pair = []
            for side in range(2):
                copy = pltpu.make_async_copy(
                    source.at[0, side, pl.ds(t * tile, tile)],
                    win.at[expert, side, pl.ds(t * tile, tile)],
                    win_sem.at[expert, side, t],
                )
                copy.start()
                pair.append(copy)
            win_copies.append(pair)
    for expert, source in enumerate((wout_a, wout_b)):
        copy = pltpu.make_async_copy(source.at[0], wout.at[expert], wout_sem.at[expert])
        copy.start()
        wout_copies.append(copy)
    for copy in copies:
        copy.wait()
    lane = lax.broadcasted_iota(jnp.int32, (ring * count, LANES), 1)
    contract = (((1,), (1,)), ((), ()))
    for expert in range(2):
        number = dev + expert - 2 * expert * lax.rem(dev, 2)
        scales = []
        for side in range(2):
            block = table_ref[side, :, first : first + count, :].reshape(half, LANES)
            scales.append(jnp.sum(jnp.where(lane == number, block, 0.0), axis=1, keepdims=True))
        scale = jnp.concatenate(scales, axis=0)
        for t in range(tiles):
            for copy in win_copies[expert * tiles + t]:
                copy.wait()
            rows = pl.ds(t * tile, tile)
            gate = lax.dot_general(
                x[...], win[expert, 0, rows, :], contract, preferred_element_type=F32
            )
            up = lax.dot_general(
                x[...], win[expert, 1, rows, :], contract, preferred_element_type=F32
            )
            value = gate / (1.0 + jnp.exp(-gate)) * up * scale
            active[expert, :, rows] = value.astype(BF)
    for copy in wout_copies:
        copy.wait()
    stores = []
    wide = min(1024, part_width)
    for side in (1, 0):
        rows = pl.ds(side * half, half)
        for begin in range(0, width, wide):
            total = jnp.dot(active[0, rows, :], wout[0, :, begin : begin + wide], preferred_element_type=F32)
            total += jnp.dot(active[1, rows, :], wout[1, :, begin : begin + wide], preferred_element_type=F32)
            stage[rows, begin : begin + wide] = total.astype(BF)
        for step in range(parts if kind == "A" else 1):
            columns = span(step) if kind == "A" else pl.ds(0, width)
            slot = side * parts + step if kind == "A" else side
            copy = pltpu.make_async_copy(stage.at[rows, columns], outs[slot], out_sem.at[slot])
            copy.start()
            stores.append(copy)
    for copy in stores:
        copy.wait()


def next_kernel(chunks, parts, place, gain_ref, w_ref, *refs):
    sub = place[0]
    out_ref, kv_ref, whole = refs[-3:]
    refs = refs[:-3]
    part_width = out_ref.shape[1]
    at = 0
    for kind, first, count in chunks:
        rows = slice(first, first + count)
        if kind == "B":
            whole[rows, :] = refs[at][...]
            at += 1
            continue
        for step in range(parts):
            begin = pl.multiple_of(part_of(sub, step, parts) * part_width, part_width)
            whole[rows, pl.ds(begin, part_width)] = refs[at][...]
            at += 1
    out_ref[...] = whole[:, pl.ds(pl.multiple_of(sub * part_width, part_width), part_width)]
    values = whole[...].astype(F32)
    scale = lax.rsqrt(jnp.mean(values * values, axis=-1, keepdims=True) + EPS)
    normed = (values * scale * gain_ref[...]).astype(BF)
    kv_ref[...] = jnp.dot(normed, w_ref[...], preferred_element_type=F32).astype(BF)


def after(value, *others):
    return lax.optimization_barrier((value,) + others)[0]


def per_device(stream_in, routes, route_weight, gain_one, gain_two, w_in, w_out, w_kv):
    tok_rows, width = stream_in.shape
    devs, parts = lax.axis_size("dev"), lax.axis_size("sub")
    ring = devs // 4
    part_width = width // parts
    hidden = w_in.shape[2]
    total = sum(size for _, size in PLAN)
    chunks, begin = [], 0
    for kind, size in PLAN:
        count = tok_rows * size // total
        chunks.append((kind, begin, count))
        begin += count
    sub, dev = lax.axis_index("sub"), lax.axis_index("dev")
    place = jnp.stack([sub, dev]).astype(jnp.int32)

    def core(value):
        return lax.ppermute(value, "dev", [(i, i ^ 1) for i in range(devs)])

    def side(value):
        return lax.ppermute(value, "dev", [(i, i ^ 2) for i in range(devs)])

    def along(value, step):
        return lax.ppermute(value, "dev", [(i, (i + 4 * step) % devs) for i in range(devs)])

    def cross(value, step):
        return lax.ppermute(value, "sub", [(i, (i + step) % parts) for i in range(parts)])

    shapes = [jax.ShapeDtypeStruct((tok_rows, LANES), F32)]
    for kind, _, count in chunks:
        if kind == "B":
            shapes.append(jax.ShapeDtypeStruct((count, width), BF))
        else:
            shapes += [jax.ShapeDtypeStruct((count, part_width), BF)] * parts
    made = pl.pallas_call(
        functools.partial(norm_kernel, chunks, parts, devs),
        out_shape=shapes,
        in_specs=[smem()] + [vmem()] * 4,
        out_specs=[vmem()] * len(shapes),
        compiler_params=params(),
        name="norm",
    )(place, stream_in, routes, route_weight, gain_one.reshape(1, width))
    table, made = made[0], list(made[1:])
    win_b, wout_b = core(w_in), core(w_out)

    gathered, held = [], None
    for index, (kind, first, count) in enumerate(chunks):
        own = made.pop(0)
        others = [made.pop(0) for _ in range(parts - 1)] if kind == "A" else []
        if held is not None:
            own = after(own, *held)
        near = [along(own, k) for k in range(1, ring)]
        held = near
        if index == 0:
            tables = [table] + [along(table, k) for k in range(1, ring)]
            tables = jnp.concatenate(tables, axis=0)
            tables = jnp.stack([tables, side(tables)]).reshape(2, ring, tok_rows, LANES)
        rest = jnp.concatenate(near, axis=0)
        if kind == "A":
            mine = jnp.concatenate([own] + near, axis=0)
            beside = side(mine)
            pieces = [mine, beside]
            for step in range(1, parts):
                pieces += [others[step - 1], cross(rest, step), cross(beside, step)]
        else:
            pieces = [jnp.concatenate([own] + near, axis=0), side(own), side(rest)]
        gathered.append(pieces)

    finished = []
    for (kind, first, count), pieces in zip(chunks, gathered):
        half = ring * count
        if kind == "A":
            outs = [jax.ShapeDtypeStruct((half, part_width), BF)] * (2 * parts)
        else:
            outs = [jax.ShapeDtypeStruct((half, width), BF)] * 2
        sums = pl.pallas_call(
            functools.partial(expert_kernel, kind, ring, count, first, parts),
            out_shape=outs,
            in_specs=[smem(), vmem()] + [hbm()] * (len(pieces) + 4),
            out_specs=[hbm()] * len(outs),
            scratch_shapes=[
                pltpu.VMEM((2 * half, width), BF),
                pltpu.VMEM((2, 2, hidden, width), BF),
                pltpu.VMEM((2, hidden, width), BF),
                pltpu.VMEM((2 * half, width), BF),
                pltpu.VMEM((2, 2 * half, hidden), BF),
                pltpu.SemaphoreType.DMA((len(pieces),)),
                pltpu.SemaphoreType.DMA((2, 2, 16)),
                pltpu.SemaphoreType.DMA((2,)),
                pltpu.SemaphoreType.DMA((len(outs),)),
            ],
            compiler_params=params(),
            name="experts",
        )(place, tables, *pieces, w_in, win_b, w_out, wout_b)
        rows = slice(first, first + count)

        def add(*values):
            return functools.reduce(lambda a, b: a + b, [v.astype(F32) for v in values])

        if kind == "A":
            near, far = sums[:parts], sums[parts:]
            far = add(far[0], *[cross(far[k], -k) for k in range(1, parts)]).astype(BF)
            beside = side(far)
            near = add(near[0], *[cross(near[k], -k) for k in range(1, parts)])
            joined = (near + beside.astype(F32)).astype(BF).reshape(ring, count, part_width)
            mixture = add(joined[0], *[along(joined[k], -k) for k in range(1, ring)])
            own = lax.dynamic_slice(stream_in, (first, sub * part_width), (count, part_width))
            own = (own.astype(F32) + mixture).astype(BF)
            finished += [own] + [cross(own, k) for k in range(1, parts)]
        else:
            joined = add(sums[0], side(sums[1])).astype(BF).reshape(ring, count, width)
            mixture = add(joined[0], *[along(joined[k], -k) for k in range(1, ring)]).astype(BF)
            mixture = add(mixture, *[cross(mixture, k) for k in range(1, parts)])
            finished.append((stream_in[rows].astype(F32) + mixture).astype(BF))

    return pl.pallas_call(
        functools.partial(next_kernel, chunks, parts),
        out_shape=[
            jax.ShapeDtypeStruct((tok_rows, part_width), BF),
            jax.ShapeDtypeStruct((tok_rows, w_kv.shape[1]), BF),
        ],
        in_specs=[smem()] + [vmem()] * (2 + len(finished)),
        out_specs=[vmem()] * 2,
        scratch_shapes=[pltpu.VMEM((tok_rows, width), BF)],
        compiler_params=params(),
        name="next_layer",
    )(place, gain_two.reshape(1, width), w_kv, *finished)


def solution(mesh):
    placed = (
        P(("groups", "dev"), None),
        P(("groups", "dev"), None),
        P(("groups", "dev"), None),
        P(),
        P(),
        P("dev", None, "sub", None),
        P("dev", "sub", None),
        P(None, "sub"),
    )

    def run(*arrays):
        return tuple(per_device(*arrays))

    return jax.shard_map(
        run,
        mesh=mesh,
        in_specs=placed,
        out_specs=(P(("groups", "dev"), "sub"), P(("groups", "dev"), "sub")),
        check_vma=False,
    )
```

```python
import functools

import jax
import jax.numpy as jnp
from jax import lax
from jax.experimental import pallas as pl
from jax.experimental.pallas import tpu as pltpu
from jax.sharding import PartitionSpec as P

EPS = 1e-06
BF = jnp.bfloat16
F32 = jnp.float32
LANES = 128
VMEM_LIMIT = 19 * 1024 * 1024


PLAN = (("A", 1), ("A", 1), ("A", 1), ("B", 1))


def vmem():
    return pl.BlockSpec(memory_space=pltpu.VMEM)


def smem():
    return pl.BlockSpec(memory_space=pltpu.SMEM)


def hbm():
    return pl.BlockSpec(memory_space=pl.ANY)


def params():
    return pltpu.CompilerParams(vmem_limit_bytes=VMEM_LIMIT)


def part_of(sub, step, parts):
    return lax.rem(sub + parts - step, parts)


def norm_kernel(chunks, parts, experts, place, x_ref, routes_ref, weight_ref, gain_ref, *outs):
    sub = place[0]
    rows, width = x_ref.shape
    part_width = width // parts
    columns = lax.broadcasted_iota(jnp.int32, (rows, LANES), 1)
    table = jnp.zeros((rows, LANES), F32)
    for k in range(routes_ref.shape[1]):
        table = table + jnp.where(routes_ref[:, k : k + 1] == columns, weight_ref[:, k : k + 1], 0.0)
    outs[0][...] = table
    at = 1
    for kind, first, count in chunks:
        values = x_ref[first : first + count, :].astype(F32)
        scale = lax.rsqrt(jnp.mean(values * values, axis=-1, keepdims=True) + EPS)
        if kind == "B":
            outs[at][...] = (values * scale * gain_ref[...]).astype(BF)
            at += 1
            continue
        for step in range(parts):
            begin = pl.multiple_of(part_of(sub, step, parts) * part_width, part_width)
            piece = x_ref[first : first + count, pl.ds(begin, part_width)].astype(F32)
            outs[at][...] = (piece * scale * gain_ref[:, pl.ds(begin, part_width)]).astype(BF)
            at += 1


def load_kernel(in_a, in_b, out_a, out_b, sems):
    copies = [
        pltpu.make_async_copy(in_a, out_a, sems.at[0]),
        pltpu.make_async_copy(in_b, out_b, sems.at[1]),
    ]
    for copy in copies:
        copy.start()
    for copy in copies:
        copy.wait()


def expert_kernel(kind, ring, count, first, parts, place, table_ref, win_a, win_b, wout_a, wout_b, *refs):
    sub, dev = place[0], place[1]
    half = ring * count
    n_in = 2 + 3 * (parts - 1) if kind == "A" else 3
    pieces, refs = refs[:n_in], refs[n_in:]
    n_out = 2 * parts if kind == "A" else 2
    outs, refs = refs[:n_out], refs[n_out:]
    x, stage, active, in_sem, out_sem = refs
    width = x.shape[1]
    part_width = width // parts

    def span(step):
        begin = pl.multiple_of(part_of(sub, step, parts) * part_width, part_width)
        return pl.ds(begin, part_width)

    copies = []

    def bring(piece, row, rows, columns):
        copy = pltpu.make_async_copy(
            piece, x.at[pl.ds(row, rows), columns], in_sem.at[len(copies)]
        )
        copy.start()
        copies.append(copy)

    if kind == "A":
        bring(pieces[0], 0, half, span(0))
        bring(pieces[1], half, half, span(0))
        for step in range(1, parts):
            own, along, across = pieces[2 + 3 * (step - 1) : 5 + 3 * (step - 1)]
            bring(own, 0, count, span(step))
            bring(along, count, half - count, span(step))
            bring(across, half, half, span(step))
    else:
        bring(pieces[0], 0, half, pl.ds(0, width))
        bring(pieces[1], half, count, pl.ds(0, width))
        bring(pieces[2], half + count, half - count, pl.ds(0, width))
    for copy in copies:
        copy.wait()
    lane = lax.broadcasted_iota(jnp.int32, (half, LANES), 1)
    contract = (((1,), (1,)), ((), ()))
    for expert, win in enumerate((win_a, win_b)):
        number = dev + expert - 2 * expert * lax.rem(dev, 2)
        scales = []
        for side in range(2):
            block = table_ref[side, :, first : first + count, :].reshape(half, LANES)
            scales.append(jnp.sum(jnp.where(lane == number, block, 0.0), axis=1, keepdims=True))
        scale = jnp.concatenate(scales, axis=0)
        hidden = win.shape[2]
        tile = 256 if hidden % 256 == 0 else 128
        for begin in range(0, hidden, tile):
            rows = slice(begin, begin + tile)
            gate = lax.dot_general(x[...], win[0, 0, rows], contract, preferred_element_type=F32)
            up = lax.dot_general(x[...], win[0, 1, rows], contract, preferred_element_type=F32)
            active[expert, :, rows] = (gate / (1.0 + jnp.exp(-gate)) * up * scale).astype(BF)
    stores = []
    wide = min(1024, part_width)
    tiles = part_width // wide
    for step in reversed(range(parts)):
        for t in range(tiles):
            begin = part_of(sub, step, parts) * part_width + t * wide
            columns = pl.ds(pl.multiple_of(begin, wide), wide)
            total = jnp.dot(active[0], wout_a[0, :, columns], preferred_element_type=F32)
            total += jnp.dot(active[1], wout_b[0, :, columns], preferred_element_type=F32)
            at = (step * tiles + t) * wide
            stage[:, at : at + wide] = total.astype(BF)
            for side in (1, 0):
                if kind == "A":
                    target = outs[side * parts + step].at[:, pl.ds(t * wide, wide)]
                else:
                    target = outs[side].at[:, columns]
                copy = pltpu.make_async_copy(
                    stage.at[pl.ds(side * half, half), pl.ds(at, wide)], target, out_sem.at[len(stores)]
                )
                copy.start()
                stores.append(copy)
    for copy in stores:
        copy.wait()


def next_kernel(chunks, parts, place, gain_ref, w_ref, *refs):
    sub = place[0]
    out_ref, kv_ref, whole = refs[-3:]
    refs = refs[:-3]
    part_width = out_ref.shape[1]
    at = 0
    for kind, first, count in chunks:
        rows = slice(first, first + count)
        if kind == "B":
            whole[rows, :] = refs[at][...]
            at += 1
            continue
        for step in range(parts):
            begin = pl.multiple_of(part_of(sub, step, parts) * part_width, part_width)
            whole[rows, pl.ds(begin, part_width)] = refs[at][...]
            at += 1
    out_ref[...] = whole[:, pl.ds(pl.multiple_of(sub * part_width, part_width), part_width)]
    values = whole[...].astype(F32)
    scale = lax.rsqrt(jnp.mean(values * values, axis=-1, keepdims=True) + EPS)
    normed = (values * scale * gain_ref[...]).astype(BF)
    kv_ref[...] = jnp.dot(normed, w_ref[...], preferred_element_type=F32).astype(BF)


def after(value, *others):
    return lax.optimization_barrier((value,) + others)[0]


def per_device(stream_in, routes, route_weight, gain_one, gain_two, w_in, w_out, w_kv):
    tok_rows, width = stream_in.shape
    devs, parts = lax.axis_size("dev"), lax.axis_size("sub")
    ring = devs // 4
    part_width = width // parts
    hidden = w_in.shape[2]
    total = sum(size for _, size in PLAN)
    chunks, begin = [], 0
    for kind, size in PLAN:
        count = tok_rows * size // total
        chunks.append((kind, begin, count))
        begin += count
    sub, dev = lax.axis_index("sub"), lax.axis_index("dev")
    place = jnp.stack([sub, dev]).astype(jnp.int32)

    def core(value):
        return lax.ppermute(value, "dev", [(i, i ^ 1) for i in range(devs)])

    def side(value):
        return lax.ppermute(value, "dev", [(i, i ^ 2) for i in range(devs)])

    def along(value, step):
        return lax.ppermute(value, "dev", [(i, (i + 4 * step) % devs) for i in range(devs)])

    def cross(value, step):
        return lax.ppermute(value, "sub", [(i, (i + step) % parts) for i in range(parts)])

    shapes = [jax.ShapeDtypeStruct((tok_rows, LANES), F32)]
    for kind, _, count in chunks:
        if kind == "B":
            shapes.append(jax.ShapeDtypeStruct((count, width), BF))
        else:
            shapes += [jax.ShapeDtypeStruct((count, part_width), BF)] * parts
    made = pl.pallas_call(
        functools.partial(norm_kernel, chunks, parts, devs),
        out_shape=shapes,
        in_specs=[smem()] + [vmem()] * 4,
        out_specs=[vmem()] * len(shapes),
        compiler_params=params(),
        name="norm",
    )(place, stream_in, routes, route_weight, gain_one.reshape(1, width))
    table, made = made[0], list(made[1:])
    win_b, wout_b = pl.pallas_call(
        load_kernel,
        out_shape=[pltpu.VMEM(w_in.shape, BF), pltpu.VMEM(w_out.shape, BF)],
        in_specs=[hbm()] * 2,
        out_specs=[vmem()] * 2,
        scratch_shapes=[pltpu.SemaphoreType.DMA((2,))],
        compiler_params=pltpu.CompilerParams(vmem_limit_bytes=1024 * 1024),
        name="load",
    )(core(w_in), core(w_out))
    weights = [
        pltpu.with_memory_space_constraint(value, pltpu.VMEM)
        for value in (w_in, win_b, w_out, wout_b)
    ]

    gathered, held, nears = [], None, []
    for index, (kind, first, count) in enumerate(chunks):
        own = made.pop(0)
        others = [made.pop(0) for _ in range(parts - 1)] if kind == "A" else []
        if held is not None:
            own = after(own, *held)
        near = [along(own, k) for k in range(1, ring)]
        held = near
        nears.append(near)
        if index == 0:
            tables = [table] + [along(table, k) for k in range(1, ring)]
            tables = jnp.concatenate(tables, axis=0)
            tables = jnp.stack([tables, side(tables)]).reshape(2, ring, tok_rows, LANES)
        rest = jnp.concatenate(near, axis=0)
        if kind == "A":
            mine = jnp.concatenate([own] + near, axis=0)
            beside = side(mine)
            pieces = [mine, beside]
            for step in range(1, parts):
                pieces += [others[step - 1], cross(rest, step), cross(beside, step)]
        else:
            pieces = [jnp.concatenate([own] + near, axis=0), side(own), side(rest)]
        gathered.append(pieces)

    def add(*values):
        return functools.reduce(lambda a, b: a + b, [v.astype(F32) for v in values])

    finished, firsts, seconds = [], [], []
    for index, ((kind, first, count), pieces) in enumerate(zip(chunks, gathered)):
        half = ring * count
        if kind == "A":
            outs = [pltpu.HBM((half, part_width), BF)] * (2 * parts)
        else:
            outs = [pltpu.HBM((half, width), BF)] * 2
        waits = []
        if index + 1 < len(chunks):
            waits += nears[index + 1]
        if index >= 2:
            waits += firsts[index - 2]
        if index >= 3:
            waits += seconds[index - 3]
        if waits:
            pieces[0] = after(pieces[0], *waits)
        sums = pl.pallas_call(
            functools.partial(expert_kernel, kind, ring, count, first, parts),
            out_shape=outs,
            in_specs=[smem()] + [vmem()] * 5 + [hbm()] * len(pieces),
            out_specs=[hbm()] * len(outs),
            scratch_shapes=[
                pltpu.VMEM((2 * half, width), BF),
                pltpu.VMEM((2 * half, width), BF),
                pltpu.VMEM((2, 2 * half, hidden), BF),
                pltpu.SemaphoreType.DMA((len(pieces),)),
                pltpu.SemaphoreType.DMA((2 * parts * max(1, part_width // 1024),)),
            ],
            compiler_params=params(),
            name="experts",
        )(place, tables, *weights, *pieces)
        rows = slice(first, first + count)
        if kind == "A":
            near, far = sums[:parts], sums[parts:]
            far_sent = [cross(far[k], -k) for k in range(1, parts)]
            near_sent = [cross(near[k], -k) for k in range(1, parts)]
            far = add(far[0], *far_sent).astype(BF)
            beside = side(far)
            near = add(near[0], *near_sent)
            joined = (near + beside.astype(F32)).astype(BF).reshape(ring, count, part_width)
            sent = [along(joined[k], -k) for k in range(1, ring)]
            mixture = add(joined[0], *sent)
            own = lax.dynamic_slice(stream_in, (first, sub * part_width), (count, part_width))
            own = (own.astype(F32) + mixture).astype(BF)
            finished += [own] + [cross(own, k) for k in range(1, parts)]
            firsts.append(far_sent)
            seconds.append([beside] + near_sent)
        else:
            beside = side(sums[1])
            joined = add(sums[0], beside).astype(BF).reshape(ring, count, width)
            sent = [along(joined[k], -k) for k in range(1, ring)]
            mixture = add(joined[0], *sent).astype(BF)
            mixture = add(mixture, *[cross(mixture, k) for k in range(1, parts)])
            finished.append((stream_in[rows].astype(F32) + mixture).astype(BF))
            firsts.append([beside])
            seconds.append(sent)

    return pl.pallas_call(
        functools.partial(next_kernel, chunks, parts),
        out_shape=[
            jax.ShapeDtypeStruct((tok_rows, part_width), BF),
            jax.ShapeDtypeStruct((tok_rows, w_kv.shape[1]), BF),
        ],
        in_specs=[smem()] + [vmem()] * (2 + len(finished)),
        out_specs=[vmem()] * 2,
        scratch_shapes=[pltpu.VMEM((tok_rows, width), BF)],
        compiler_params=params(),
        name="next_layer",
    )(place, gain_two.reshape(1, width), w_kv, *finished)


def solution(mesh):
    placed = (
        P(("groups", "dev"), None),
        P(("groups", "dev"), None),
        P(("groups", "dev"), None),
        P(),
        P(),
        P("dev", None, "sub", None),
        P("dev", "sub", None),
        P(None, "sub"),
    )

    def run(*arrays):
        return tuple(per_device(*arrays))

    return jax.shard_map(
        run,
        mesh=mesh,
        in_specs=placed,
        out_specs=(P(("groups", "dev"), "sub"), P(("groups", "dev"), "sub")),
        check_vma=False,
    )
```

```python
import functools

import jax
import jax.numpy as jnp
from jax import lax
from jax.experimental import pallas as pl
from jax.experimental.pallas import tpu as pltpu
from jax.sharding import PartitionSpec as P


EPS = 1e-06
BF = jnp.bfloat16
F32 = jnp.float32
VMEM_LIMIT = 48 * 1024 * 1024
AHEAD = 3


PLAN = (("A", "A", 4), ("A", "A", 6), ("B", "B", 4), ("B", "A", 2))


def vmem():
    return pl.BlockSpec(memory_space=pltpu.VMEM)


def smem():
    return pl.BlockSpec(memory_space=pltpu.SMEM)


def hbm():
    return pl.BlockSpec(memory_space=pl.ANY)


def params():
    return pltpu.CompilerParams(vmem_limit_bytes=VMEM_LIMIT)


def part_of(sub, step, parts):
    return lax.rem(sub + parts - step, parts)


def norm_kernel(chunks, parts, place, x_ref, routes_ref, weight_ref, gain_ref, *outs):
    sub = place[0]
    _, width = x_ref.shape
    part_width = width // parts
    number = lax.broadcasted_iota(jnp.int32, outs[0].shape, 0)
    table = jnp.zeros(outs[0].shape, F32)
    for k in range(routes_ref.shape[0]):
        table = table + jnp.where(routes_ref[k : k + 1, :] == number, weight_ref[k : k + 1, :], 0.0)
    outs[0][...] = table
    for out, (kind, _, first, count) in zip(outs[1:], chunks):
        values = x_ref[first : first + count, :].astype(F32)
        scale = lax.rsqrt(jnp.mean(values * values, axis=-1, keepdims=True) + EPS)
        if kind == "B":
            out[...] = (values * scale * gain_ref[...]).astype(BF)
        else:
            columns = pl.ds(pl.multiple_of(sub * part_width, part_width), part_width)
            piece = x_ref[first : first + count, columns].astype(F32)
            out[...] = (piece * scale * gain_ref[:, columns]).astype(BF)


def expert_kernel(kinds, first, count, parts, place, table_ref, win_a, win_b, wout_a, wout_b, *refs):
    sub, dev = place[0], place[1]
    gather, reduce = kinds
    n_in = 2 * parts if gather == "A" else 2
    pieces, refs = refs[:n_in], refs[n_in:]
    n_out = 2 * parts if reduce == "A" else 2
    outs, refs = refs[:n_out], refs[n_out:]
    x, active, win, wout, in_sem, weight_sem, out_sem = refs
    stage = x
    rows, width = x.shape
    half = rows // 2
    part_width = width // parts

    copies = []
    for at, piece in enumerate(pieces):
        columns = pl.ds(0, width)
        if gather == "A":
            begin = part_of(sub, at // 2, parts) * part_width
            columns = pl.ds(pl.multiple_of(begin, part_width), part_width)
        copy = pltpu.make_async_copy(piece, x.at[pl.ds(at % 2 * half, half), columns], in_sem.at[at])
        copy.start()
        copies.append(copy)
    hidden = active.shape[2]
    tile = 256 if hidden % 256 == 0 else 128
    wide = min(1024, part_width)
    spans = [(expert, slice(begin, begin + tile)) for expert in range(2) for begin in range(0, hidden, tile)]
    tiles = part_width // wide
    steps = [(step, t) for step in reversed(range(parts)) for t in range(tiles)]

    def columns_of(step, t):
        begin = part_of(sub, step, parts) * part_width + t * wide
        return pl.ds(pl.multiple_of(begin, wide), wide)

    stages = []
    for expert, span in spans:
        source = (win_a, win_b)[expert]
        stages.append([(source.at[0, side, span], win.at[expert, side, span]) for side in range(2)])
    for step, t in steps:
        columns = columns_of(step, t)
        stages.append(
            [(source.at[0, :, columns], wout.at[expert, :, columns]) for expert, source in enumerate((wout_a, wout_b))]
        )
    fetches = [
        [pltpu.make_async_copy(*pair, weight_sem.at[at, k]) for k, pair in enumerate(stage)]
        for at, stage in enumerate(stages)
    ]

    def begin_fetch(at):
        for copy in fetches[at] if at < len(fetches) else []:
            copy.start()

    def end_fetch(at):
        begin_fetch(at + AHEAD)
        for copy in fetches[at]:
            copy.wait()

    assert hidden // tile == AHEAD <= len(steps)
    for at in range(AHEAD):
        begin_fetch(at)
    for copy in copies:
        copy.wait()
    contract = (((1,), (1,)), ((), ()))
    table = table_ref[...].T[first : first + count, :]
    slots = rows // count
    experts = table.shape[1] // slots
    lane = lax.broadcasted_iota(jnp.int32, table.shape, 1)
    scales = []
    for expert in range(2):
        number = dev + expert - 2 * expert * lax.rem(dev, 2)
        picked = [
            jnp.sum(jnp.where(lane == number + slot * experts, table, 0.0), axis=1, keepdims=True)
            for slot in range(slots)
        ]
        scales.append(jnp.concatenate(picked, axis=0))
    per_expert = hidden // tile
    for expert in range(2):

        def hidden_tile(t, carry):
            span = pl.ds(pl.multiple_of(t * tile, tile), tile)
            ahead = []
            if expert == 0:
                for side in range(2):
                    ahead.append((win_b.at[0, side, span], win.at[1, side, span], per_expert + t, side))
            else:
                begin = part_of(sub, parts - 1 - t // tiles, parts) * part_width + lax.rem(t, tiles) * wide
                columns = pl.ds(pl.multiple_of(begin, wide), wide)
                for which, source in enumerate((wout_a, wout_b)):
                    ahead.append((source.at[0, :, columns], wout.at[which, :, columns], 2 * per_expert + t, which))
            for source, target, number, which in ahead:
                pltpu.make_async_copy(source, target, weight_sem.at[number, which]).start()
            for side in range(2):
                pltpu.make_async_copy(
                    win_a.at[0, side, span], win.at[expert, side, span], weight_sem.at[expert * per_expert + t, side]
                ).wait()
            gate = lax.dot_general(x[...], win[expert, 0, span], contract, preferred_element_type=F32)
            up = lax.dot_general(x[...], win[expert, 1, span], contract, preferred_element_type=F32)
            active[expert, :, span] = (gate / (1.0 + jnp.exp(-gate)) * up * scales[expert]).astype(BF)
            return carry

        lax.fori_loop(0, per_expert, hidden_tile, 0)
    stores = []
    for number, (step, t) in enumerate(steps):
        end_fetch(len(spans) + number)
        columns = columns_of(step, t)
        total = jnp.dot(active[0], wout[0, :, columns], preferred_element_type=F32)
        total += jnp.dot(active[1], wout[1, :, columns], preferred_element_type=F32)
        at = (step * tiles + t) * wide
        stage[:, at : at + wide] = total.astype(BF)
        for side in (1, 0):
            if reduce == "A":
                target = outs[side * parts + step].at[:, pl.ds(t * wide, wide)]
            else:
                target = outs[side].at[:, columns]
            copy = pltpu.make_async_copy(
                stage.at[pl.ds(side * half, half), pl.ds(at, wide)], target, out_sem.at[len(stores)]
            )
            copy.start()
            stores.append(copy)
    for copy in stores:
        copy.wait()


def next_kernel(chunks, parts, place, gain_ref, w_ref, *refs):
    sub = place[0]
    out_ref, kv_ref, whole = refs[-3:]
    refs = refs[:-3]
    part_width = out_ref.shape[1]
    at = 0
    for _, kind, first, count in chunks:
        rows = slice(first, first + count)
        if kind == "B":
            whole[rows, :] = refs[at][...]
            at += 1
            continue
        for step in range(parts):
            begin = pl.multiple_of(part_of(sub, step, parts) * part_width, part_width)
            whole[rows, pl.ds(begin, part_width)] = refs[at][...]
            at += 1
    out_ref[...] = whole[:, pl.ds(pl.multiple_of(sub * part_width, part_width), part_width)]
    values = whole[...].astype(F32)
    scale = lax.rsqrt(jnp.mean(values * values, axis=-1, keepdims=True) + EPS)
    normed = (values * scale * gain_ref[...]).astype(BF)
    kv_ref[...] = jnp.dot(normed, w_ref[...], preferred_element_type=F32).astype(BF)


def per_device(stream_in, routes, route_weight, gain_one, gain_two, w_in, w_out, w_kv):
    tok_rows, width = stream_in.shape
    devs, parts = lax.axis_size("dev"), lax.axis_size("sub")
    part_width = width // parts
    hidden = w_in.shape[2]
    total = sum(entry[2] for entry in PLAN)
    chunks, begin = [], 0
    for gather, reduce, size in PLAN:
        count = tok_rows * size // total
        chunks.append((gather, reduce, begin, count))
        begin += count
    bits = []
    while devs >> (len(bits) + 2):
        bits.insert(0, 2 << len(bits))
    sub, dev = lax.axis_index("sub"), lax.axis_index("dev")
    place = jnp.stack([sub, dev]).astype(jnp.int32)

    def swap(value, bit):
        return lax.ppermute(value, "dev", [(i, i ^ bit) for i in range(devs)])

    def cross(value, step):
        return lax.ppermute(value, "sub", [(i, (i + step) % parts) for i in range(parts)])

    def add(*values):
        return functools.reduce(lambda a, b: a + b, [v.astype(F32) for v in values])

    shapes = [jax.ShapeDtypeStruct((devs, tok_rows), F32)]
    for gather, _, _, count in chunks:
        shapes.append(jax.ShapeDtypeStruct((count, width if gather == "B" else part_width), BF))
    table, *owns = pl.pallas_call(
        functools.partial(norm_kernel, chunks, parts),
        out_shape=shapes,
        in_specs=[smem()] + [vmem()] * 4,
        out_specs=[vmem()] * len(shapes),
        compiler_params=params(),
        name="norm",
    )(place, stream_in, routes.T, route_weight.T, gain_one.reshape(1, width))
    weights = [w_in, swap(w_in, 1), w_out, swap(w_out, 1)]
    for bit in bits:
        table = jnp.concatenate([table, swap(table, bit)], axis=0)
    gathered = []
    for index, (gather, _, first, count) in enumerate(chunks):
        held = owns[index]
        for bit in bits[:-1]:
            got = swap(held, bit)
            held = jnp.concatenate([held, got], axis=0)
        beside = swap(held, bits[-1])
        pieces = [held, beside]
        if gather == "A":
            for step in range(1, parts):
                pieces += [cross(held, step), cross(beside, step)]
        gathered.append(pieces)

    finished = []
    for (gather, reduce, first, count), pieces in zip(chunks, gathered):
        rows = devs // 2 * count
        half = rows // 2
        if reduce == "A":
            outs = [pltpu.HBM((half, part_width), BF)] * (2 * parts)
        else:
            outs = [pltpu.HBM((half, width), BF)] * 2
        call = pl.pallas_call(
            functools.partial(expert_kernel, (gather, reduce), first, count, parts),
            out_shape=outs,
            in_specs=[smem(), vmem()] + [hbm()] * (4 + len(pieces)),
            out_specs=[hbm()] * len(outs),
            scratch_shapes=[
                pltpu.VMEM((rows, width), BF),
                pltpu.VMEM((2, rows, hidden), BF),
                pltpu.VMEM((2, 2, hidden, width), BF),
                pltpu.VMEM((2, hidden, width), BF),
                pltpu.SemaphoreType.DMA((len(pieces),)),
                pltpu.SemaphoreType.DMA((32, 2)),
                pltpu.SemaphoreType.DMA((2 * parts * max(1, part_width // 1024),)),
            ],
            compiler_params=params(),
            name="experts",
        )
        sums = call(place, table, *weights, *pieces)
        if reduce == "A":
            near, far = sums[:parts], sums[parts:]
            far = add(far[0], *[cross(far[k], -k) for k in range(1, parts)])
            near_sent = [cross(near[k], -k) for k in range(1, parts)]
            beside = swap(far.astype(BF), bits[-1])
            held = add(near[0], *near_sent, beside)
        else:
            held = add(sums[0], swap(sums[1], bits[-1]))
        for bit in reversed(bits[:-1]):
            middle = held.shape[0] // 2
            got = swap(held[middle:].astype(BF), bit)
            held = held[:middle] + got.astype(F32)
        if reduce == "A":
            own = lax.dynamic_slice(stream_in, (first, sub * part_width), (count, part_width))
            own = (own.astype(F32) + held).astype(BF)
            finished += [own] + [cross(own, k) for k in range(1, parts)]
        else:
            mixture = held.astype(BF)
            mixture = add(mixture, *[cross(mixture, k) for k in range(1, parts)])
            finished.append((stream_in[first : first + count].astype(F32) + mixture).astype(BF))

    return pl.pallas_call(
        functools.partial(next_kernel, chunks, parts),
        out_shape=[
            jax.ShapeDtypeStruct((tok_rows, part_width), BF),
            jax.ShapeDtypeStruct((tok_rows, w_kv.shape[1]), BF),
        ],
        in_specs=[smem()] + [vmem()] * (2 + len(finished)),
        out_specs=[vmem()] * 2,
        scratch_shapes=[pltpu.VMEM((tok_rows, width), BF)],
        compiler_params=params(),
        name="next_layer",
    )(place, gain_two.reshape(1, width), w_kv, *finished)


def solution(mesh):
    placed = (
        P(("groups", "dev"), None),
        P(("groups", "dev"), None),
        P(("groups", "dev"), None),
        P(),
        P(),
        P("dev", None, "sub", None),
        P("dev", "sub", None),
        P(None, "sub"),
    )

    def run(*arrays):
        return tuple(per_device(*arrays))

    return jax.shard_map(
        run,
        mesh=mesh,
        in_specs=placed,
        out_specs=(P(("groups", "dev"), "sub"), P(("groups", "dev"), "sub")),
        check_vma=False,
    )
```
